32 devices in a mesh: obs: 16 (over z, x, core), sp: 2 (over y).
Axes of the slice: x: 2, y: 2, z: 4, core: 2. Of those that a mesh axis runs over, the one named last changes fastest.
Arguments:
- descriptors: bfloat16 [16384, 512], P('obs'), may hold values from -10 to 10
- candidates: bfloat16 [8192, 512], P('obs'), may hold values from -10 to 10
- sparse_index: int32 [4096], replicated, may hold values from 0 to 8191, as said below
- targets: bfloat16 [16384], P('obs'), may hold values from -12 to 12
- regularizer: float32 [4096], replicated, may hold values from 0.25 to 1
Outputs:
- inverse: float32 [4096, 4096], P('sp', 'obs')
- weights: float32 [4096], P('sp')
The draws below stay inside these ranges and needn't reach their ends.
Inputs may be any that keep to these rules, and one draw needn't show every extreme that they name: `sparse_index`: the 4096 indices are distinct.
All inputs are finite; a program needn't handle non-finite values.
Results may differ from the reference program's by a relative error of at most 0.012.
Values may be sent and summed in bfloat16 or wider, within the bound.
A program may use at most 128 MiB of HBM per device.

```python
import math
import jax
import jax.numpy as jnp
from jax import lax

D = 512
M = 4096
OBS_DEV = 1024
ROWS = 16384
CAND = 8192
N_OBS = 16


def draw_descriptors(key, part):
    own_key = jax.random.fold_in(key, 31)
    values = jnp.clip(jax.random.normal(own_key, (ROWS, D), jnp.float32), -6.0, 6.0)
    return values.astype(jnp.bfloat16)


def draw_candidates(key, part):
    own_key = jax.random.fold_in(key, 72)
    values = jnp.clip(jax.random.normal(own_key, (CAND, D), jnp.float32), -6.0, 6.0)
    return values.astype(jnp.bfloat16)


def draw_sparse_index(key, part):
    own_key = jax.random.fold_in(key, 17)
    return jax.random.permutation(own_key, CAND)[:M].astype(jnp.int32)


def draw_targets(key, part):
    own_key = jax.random.fold_in(key, 53)
    ramp_up = 1.0 + 2.0 * jnp.arange(ROWS, dtype=jnp.float32) / ROWS
    values = jnp.clip(jax.random.normal(own_key, (ROWS,), jnp.float32), -4.0, 4.0)
    return (values * ramp_up).astype(jnp.bfloat16)


def setup_inputs(seed: int = 0) -> dict:
    arg_keys = jax.random.split(jax.random.key(seed), 6)
    descriptors = draw_descriptors(jax.random.fold_in(arg_keys[5], 71), 0)
    candidates = draw_candidates(jax.random.fold_in(arg_keys[5], 71), 0)
    sparse_index = draw_sparse_index(jax.random.fold_in(arg_keys[5], 71), 0)
    targets = draw_targets(jax.random.fold_in(arg_keys[5], 71), 0)
    regularizer = jnp.clip(jnp.exp(jax.random.uniform(arg_keys[4], (M,), jnp.float32, math.log(0.25), math.log(1.0))), 0.25, 1.0)
    return {"descriptors": descriptors, "candidates": candidates, "sparse_index": sparse_index, "targets": targets, "regularizer": regularizer}


epsilon = 1e-06

def unit_rows(row_block):
    values = row_block.astype(jnp.float32)
    return (values * lax.rsqrt(lax.optimization_barrier(jnp.sum(values * values, axis=1, keepdims=True)) + epsilon)).astype(jnp.bfloat16)

def kernel_block(normed, sparse):
    inner = lax.dot_general(normed, sparse, (((1,), (1,)), ((), ())), preferred_element_type=jnp.float32)
    scaled = inner * math.sqrt(normed.shape[1])
    squared = scaled * scaled
    return (squared * squared - 6.0 * squared + 3.0).astype(jnp.bfloat16)

def reference(descriptors, candidates, sparse_index, targets, regularizer):
    normed = unit_rows(descriptors)
    sparse = unit_rows(candidates)[sparse_index]

    def accumulate(running, begin_at):
        gram_sum, weighted = running
        row_block = lax.dynamic_slice_in_dim(normed, begin_at, OBS_DEV)
        values = lax.dynamic_slice_in_dim(targets, begin_at, OBS_DEV)
        block_kernel = kernel_block(row_block, sparse)
        gram_sum = gram_sum + lax.dot_general(block_kernel, block_kernel, (((0,), (0,)), ((), ())), preferred_element_type=jnp.float32)
        weighted = weighted + jnp.dot(values, block_kernel, preferred_element_type=jnp.float32)
        return ((gram_sum, weighted), None)
    starts = (jnp.arange(N_OBS) * OBS_DEV).astype(jnp.int32)
    initial = (jnp.zeros((M, M), jnp.float32), jnp.zeros((M,), jnp.float32))
    (gram_sum, weighted), _ = lax.scan(accumulate, initial, starts)
    normalizer = 24.0 * ROWS
    projected = weighted / math.sqrt(normalizer)
    system = gram_sum / normalizer + jnp.diag(regularizer)
    recip = 1.0 / jnp.diagonal(system)
    first = jnp.diag(2.0 * recip) - system * recip[:, None] * recip[None, :]
    highest = lax.Precision.HIGHEST
    product = jnp.dot(system, first, precision=highest)
    inverse = 2.0 * first - jnp.dot(first, product, precision=highest)
    weights = jnp.dot(inverse, projected, precision=highest)
    return (inverse, weights)
```

```python
import functools
import math

import jax
import jax.numpy as jnp
from jax import lax
from jax.experimental import pallas as pl
from jax.experimental.pallas import tpu as pltpu
from jax.sharding import PartitionSpec as P

epsilon = 1e-06
LANES = 128
VMEM_BYTES = 58 * 2**20


def unit_rows(row_block):
    values = row_block.astype(jnp.float32)
    return (values * lax.rsqrt(jnp.sum(values * values, axis=1, keepdims=True) + epsilon)).astype(
        jnp.bfloat16
    )


def gram_body(blocks, tile, share, ext, root, s_ref, norm_ref, sp_ref, tgt_ref, gram_ref, ws_ref, kext):
    step = pl.program_id(0)
    width = blocks * tile

    @pl.when(step < blocks)
    def _():
        inner = lax.dot_general(
            norm_ref[...], sp_ref[...], (((1,), (1,)), ((), ())), preferred_element_type=jnp.float32
        )
        scaled = inner * root
        squared = scaled * scaled
        kb = ((squared - 6.0) * squared + 3.0).astype(jnp.bfloat16)
        kext[:, pl.ds(pl.multiple_of(step * tile, tile), tile)] = kb

        @pl.when(step < ext)
        def _():
            kext[:, pl.ds(pl.multiple_of(width + step * tile, tile), tile)] = kb

        kf = kb.astype(jnp.float32)
        weighted = jnp.dot(tgt_ref[...], kb, preferred_element_type=jnp.float32)
        ws_ref[0:1, :] = weighted[0:1, :]
        ws_ref[1:2, :] = jnp.sum(kf * kf, axis=0, keepdims=True)

    @pl.when(step >= blocks)
    def _():
        j = step - blocks
        cols = pl.ds(pl.multiple_of(j * tile, tile), tile)
        window = pl.ds(pl.multiple_of(j * tile + s_ref[0] * share, LANES), share)
        gram_ref[...] = lax.dot_general(
            kext[:, cols], kext[:, window], (((0,), (0,)), ((), ())), preferred_element_type=jnp.float32
        ).astype(jnp.bfloat16)


def gram_call(s_pos, normed, sparse, targets, blocks, tile, share, sp_count):
    rows, depth = normed.shape
    width = blocks * tile
    ext = -(-((blocks - 1) * tile + sp_count * share - width) // tile)
    last = blocks - 1
    return pl.pallas_call(
        functools.partial(gram_body, blocks, tile, share, ext, math.sqrt(depth)),
        grid_spec=pltpu.PrefetchScalarGridSpec(
            num_scalar_prefetch=1,
            grid=(2 * blocks,),
            in_specs=[
                pl.BlockSpec((rows, depth), lambda g, s: (0, 0)),
                pl.BlockSpec((tile, depth), lambda g, s: (jnp.minimum(g, last), 0)),
                pl.BlockSpec((16, rows), lambda g, s: (0, 0)),
            ],
            out_specs=[
                pl.BlockSpec((tile, share), lambda g, s: (jnp.maximum(g - blocks, 0), 0)),
                pl.BlockSpec((2, tile), lambda g, s: (0, jnp.minimum(g, last))),
            ],
            scratch_shapes=[pltpu.VMEM((rows, width + ext * tile), jnp.bfloat16)],
        ),
        out_shape=[
            jax.ShapeDtypeStruct((width, share), jnp.bfloat16),
            jax.ShapeDtypeStruct((2, width), jnp.float32),
        ],
        compiler_params=pltpu.CompilerParams(vmem_limit_bytes=VMEM_BYTES),
    )(s_pos, normed, sparse, jnp.broadcast_to(targets[None, :], (16, rows)))


def newton_body(
    blocks, tile, share, sp_count, chunk, block_rows,
    pos_ref, packed_ref, rcol_ref, rrow_ref, y_ref, inv_ref, w_ref, dense, prod,
):
    step = pl.program_id(0)
    width = blocks * tile
    half = blocks // 2
    p_steps = width // chunk
    my_cols = pl.ds(pl.multiple_of(pos_ref[1] * tile, tile), tile)

    @pl.when(step < blocks)
    def _():
        rows = pl.ds(pl.multiple_of(step * tile, tile), tile)
        for s in range(sp_count):
            for q in range(share // LANES):
                offset = s * share + q * LANES
                if offset >= (half + 1) * tile:
                    continue
                col = lax.rem(step * tile + offset, width)
                cols = pl.ds(pl.multiple_of(col, LANES), LANES)
                block = packed_ref[s * tile : (s + 1) * tile, q * LANES : (q + 1) * LANES]
                dense[rows, cols] = block
                if tile <= offset < half * tile:
                    dense[cols, rows] = block.T

    @pl.when((step >= blocks) & (step < blocks + p_steps))
    def _():
        rows = pl.ds(pl.multiple_of((step - blocks) * chunk, chunk), chunk)
        prod[rows, :] = jnp.dot(
            dense[rows, :], dense[:, my_cols], preferred_element_type=jnp.float32
        ).astype(jnp.bfloat16)

    @pl.when(step >= blocks + p_steps)
    def _():
        local = pl.multiple_of((step - blocks - p_steps) * chunk, chunk)
        start = pl.multiple_of(pos_ref[0] * block_rows + local, chunk)
        rows = pl.ds(start, chunk)
        cubic = jnp.dot(dense[rows, :], prod[...], preferred_element_type=jnp.float32)
        on_diag = (start + lax.broadcasted_iota(jnp.int32, (chunk, tile), 0)) == (
            pos_ref[1] * tile + lax.broadcasted_iota(jnp.int32, (chunk, tile), 1)
        )
        series = (
            jnp.where(on_diag, 1.0, 0.0)
            - dense[rows, my_cols].astype(jnp.float32)
            + prod[rows, :].astype(jnp.float32)
            - cubic
        )
        out = series * rcol_ref[rows, :] * rrow_ref[...]
        inv_ref[pl.ds(local, chunk), :] = out
        w_ref[:, pl.ds(local, chunk)] = lax.dot_general(
            y_ref[...], out, (((1,), (1,)), ((), ())),
            precision=lax.Precision.HIGHEST, preferred_element_type=jnp.float32,
        )


def newton_call(pos, packed, root_recip, rrow, y, blocks, tile, share, sp_count):
    width = blocks * tile
    block_rows = width // sp_count
    chunk = min(512, block_rows)
    grid = blocks + width // chunk + block_rows // chunk
    last = blocks - 1
    return pl.pallas_call(
        functools.partial(newton_body, blocks, tile, share, sp_count, chunk, block_rows),
        grid_spec=pltpu.PrefetchScalarGridSpec(
            num_scalar_prefetch=1,
            grid=(grid,),
            in_specs=[
                pl.BlockSpec((sp_count * tile, share), lambda g, p: (jnp.minimum(g, last), 0)),
                pl.BlockSpec((width, 1), lambda g, p: (0, 0)),
                pl.BlockSpec((1, tile), lambda g, p: (0, 0)),
                pl.BlockSpec((8, tile), lambda g, p: (0, 0)),
            ],
            out_specs=[
                pl.BlockSpec((block_rows, tile), lambda g, p: (0, 0)),
                pl.BlockSpec((8, block_rows), lambda g, p: (0, 0)),
            ],
            scratch_shapes=[
                pltpu.VMEM((width, width), jnp.bfloat16),
                pltpu.VMEM((width, tile), jnp.bfloat16),
            ],
        ),
        out_shape=[
            jax.ShapeDtypeStruct((block_rows, tile), jnp.float32),
            jax.ShapeDtypeStruct((8, block_rows), jnp.float32),
        ],
        compiler_params=pltpu.CompilerParams(vmem_limit_bytes=VMEM_BYTES),
    )(pos, packed, root_recip[:, None], rrow[None, :], jnp.broadcast_to(y[None, :], (8, tile)))


def on_device(descriptors, candidates, sparse_index, targets, regularizer):
    obs_count = lax.axis_size("obs")
    sp_count = lax.axis_size("sp")
    obs_pos = lax.axis_index("obs")
    sp_pos = lax.axis_index("sp")
    width = sparse_index.shape[0]
    tile = width // obs_count
    share = -(-((obs_count // 2 + 1) * tile) // (sp_count * LANES)) * LANES
    normalizer = 24.0 * descriptors.shape[0] * obs_count

    normed = unit_rows(descriptors)
    piece = candidates.shape[0] // sp_count
    own = lax.dynamic_slice_in_dim(candidates, sp_pos * piece, piece)
    table = lax.all_gather(unit_rows(own), ("obs", "sp"), axis=0, tiled=True)
    sparse = table.at[sparse_index].get(mode="promise_in_bounds")

    gram, sums = gram_call(
        sp_pos[None].astype(jnp.int32), normed, sparse, targets, obs_count, tile, share, sp_count
    )
    sums = lax.psum(sums, "obs")
    gram, sums = lax.optimization_barrier((gram, sums))
    part = lax.psum_scatter(gram, "obs", scatter_dimension=0, tiled=True)

    projected = sums[0] / math.sqrt(normalizer)
    root = lax.rsqrt(sums[1] / normalizer + regularizer)
    col_start = obs_pos * tile
    rrow = lax.dynamic_slice_in_dim(root, col_start, tile)
    window_start = col_start + sp_pos * share
    rwin = lax.dynamic_slice_in_dim(jnp.concatenate([root, root]), window_start, share)
    offset = sp_pos * share + lax.iota(jnp.int32, share)
    on_diag = lax.iota(jnp.int32, tile)[:, None] == offset[None, :]
    scaled = jnp.where(
        on_diag, 0.0, part.astype(jnp.float32) * (rrow[:, None] / normalizer) * rwin[None, :]
    ).astype(jnp.bfloat16)
    packed = lax.all_gather(scaled, ("obs", "sp"), axis=0, tiled=True)

    y = lax.dynamic_slice_in_dim(projected, col_start, tile)
    pos = jnp.stack([sp_pos, obs_pos]).astype(jnp.int32)
    inverse_tile, part_w = newton_call(
        pos, packed, root, rrow, y, obs_count, tile, share, sp_count
    )
    return inverse_tile, lax.psum(part_w[0], "obs")


def solution(mesh):
    in_specs = (P("obs", None), P("obs", None), P(), P("obs"), P())
    out_specs = (P("sp", "obs"), P("sp"))
    return jax.shard_map(
        on_device, mesh=mesh, in_specs=in_specs, out_specs=out_specs, check_vma=False
    )
```

```python
import functools
import math

import jax
import jax.numpy as jnp
from jax import lax
from jax.experimental import pallas as pl
from jax.experimental.pallas import tpu as pltpu
from jax.sharding import PartitionSpec as P

epsilon = 1e-06
LANES = 128
VMEM_BYTES = 58 * 2**20


def unit_rows(row_block):
    values = row_block.astype(jnp.float32)
    return (values * lax.rsqrt(jnp.sum(values * values, axis=1, keepdims=True) + epsilon)).astype(
        jnp.bfloat16
    )


def gram_body(blocks, tile, share, ext, root, s_ref, norm_ref, sp_ref, tgt_ref, gram_ref, ws_ref, kext):
    step = pl.program_id(0)
    width = blocks * tile

    @pl.when(step < blocks)
    def _():
        inner = lax.dot_general(
            norm_ref[...], sp_ref[...], (((1,), (1,)), ((), ())), preferred_element_type=jnp.float32
        )
        scaled = inner * root
        squared = scaled * scaled
        kb = ((squared - 6.0) * squared + 3.0).astype(jnp.bfloat16)
        kext[:, pl.ds(pl.multiple_of(step * tile, tile), tile)] = kb

        @pl.when(step < ext)
        def _():
            kext[:, pl.ds(pl.multiple_of(width + step * tile, tile), tile)] = kb

        kf = kb.astype(jnp.float32)
        weighted = jnp.dot(tgt_ref[...], kb, preferred_element_type=jnp.float32)
        ws_ref[0:1, :] = weighted[0:1, :]
        ws_ref[1:2, :] = jnp.sum(kf * kf, axis=0, keepdims=True)

    @pl.when(step >= blocks)
    def _():
        j = step - blocks
        cols = pl.ds(pl.multiple_of(j * tile, tile), tile)
        window = pl.ds(pl.multiple_of(j * tile + s_ref[0] * share, LANES), share)
        gram_ref[...] = lax.dot_general(
            kext[:, cols], kext[:, window], (((0,), (0,)), ((), ())), preferred_element_type=jnp.float32
        ).astype(jnp.bfloat16)


def gram_call(s_pos, normed, sparse, targets, blocks, tile, share, sp_count):
    rows, depth = normed.shape
    width = blocks * tile
    ext = -(-((blocks - 1) * tile + sp_count * share - width) // tile)
    last = blocks - 1
    return pl.pallas_call(
        functools.partial(gram_body, blocks, tile, share, ext, math.sqrt(depth)),
        grid_spec=pltpu.PrefetchScalarGridSpec(
            num_scalar_prefetch=1,
            grid=(2 * blocks,),
            in_specs=[
                pl.BlockSpec((rows, depth), lambda g, s: (0, 0)),
                pl.BlockSpec((tile, depth), lambda g, s: (jnp.minimum(g, last), 0)),
                pl.BlockSpec((16, rows), lambda g, s: (0, 0)),
            ],
            out_specs=[
                pl.BlockSpec((tile, share), lambda g, s: (jnp.maximum(g - blocks, 0), 0)),
                pl.BlockSpec((2, tile), lambda g, s: (0, jnp.minimum(g, last))),
            ],
            scratch_shapes=[pltpu.VMEM((rows, width + ext * tile), jnp.bfloat16)],
        ),
        out_shape=[
            jax.ShapeDtypeStruct((width, share), jnp.bfloat16),
            jax.ShapeDtypeStruct((2, width), jnp.float32),
        ],
        compiler_params=pltpu.CompilerParams(vmem_limit_bytes=VMEM_BYTES),
    )(s_pos, normed, sparse, jnp.broadcast_to(targets[None, :], (16, rows)))


def newton_body(
    blocks, tile, share, sp_count, chunk, block_rows,
    pos_ref, packed_ref, rcol_ref, rrow_ref, y_ref, inv_ref, w_ref, dense, prod,
):
    step = pl.program_id(0)
    width = blocks * tile
    half = blocks // 2
    p_steps = width // chunk
    my_cols = pl.ds(pl.multiple_of(pos_ref[1] * tile, tile), tile)

    @pl.when(step < blocks)
    def _():
        rows = pl.ds(pl.multiple_of(step * tile, tile), tile)
        for s in range(sp_count):
            for q in range(share // LANES):
                offset = s * share + q * LANES
                if offset >= (half + 1) * tile:
                    continue
                col = lax.rem(step * tile + offset, width)
                cols = pl.ds(pl.multiple_of(col, LANES), LANES)
                block = packed_ref[s * tile : (s + 1) * tile, q * LANES : (q + 1) * LANES]
                dense[rows, cols] = block
                if tile <= offset < half * tile:
                    dense[cols, rows] = block.T

    @pl.when((step >= blocks) & (step < blocks + p_steps))
    def _():
        rows = pl.ds(pl.multiple_of((step - blocks) * chunk, chunk), chunk)
        prod[rows, :] = jnp.dot(
            dense[rows, :], dense[:, my_cols], preferred_element_type=jnp.float32
        ).astype(jnp.bfloat16)

    @pl.when(step >= blocks + p_steps)
    def _():
        local = pl.multiple_of((step - blocks - p_steps) * chunk, chunk)
        start = pl.multiple_of(pos_ref[0] * block_rows + local, chunk)
        rows = pl.ds(start, chunk)
        cubic = jnp.dot(dense[rows, :], prod[...], preferred_element_type=jnp.float32)
        on_diag = (start + lax.broadcasted_iota(jnp.int32, (chunk, tile), 0)) == (
            pos_ref[1] * tile + lax.broadcasted_iota(jnp.int32, (chunk, tile), 1)
        )
        series = (
            jnp.where(on_diag, 1.0, 0.0)
            - dense[rows, my_cols].astype(jnp.float32)
            + prod[rows, :].astype(jnp.float32)
            - cubic
        )
        out = series * rcol_ref[rows, :] * rrow_ref[...]
        inv_ref[pl.ds(local, chunk), :] = out
        w_ref[:, pl.ds(local, chunk)] = lax.dot_general(
            y_ref[...], out, (((1,), (1,)), ((), ())),
            precision=lax.Precision.HIGHEST, preferred_element_type=jnp.float32,
        )


def newton_call(pos, packed, root_recip, rrow, y, blocks, tile, share, sp_count):
    width = blocks * tile
    block_rows = width // sp_count
    chunk = min(512, block_rows)
    grid = blocks + width // chunk + block_rows // chunk
    last = blocks - 1
    return pl.pallas_call(
        functools.partial(newton_body, blocks, tile, share, sp_count, chunk, block_rows),
        grid_spec=pltpu.PrefetchScalarGridSpec(
            num_scalar_prefetch=1,
            grid=(grid,),
            in_specs=[
                pl.BlockSpec((sp_count * tile, share), lambda g, p: (jnp.minimum(g, last), 0)),
                pl.BlockSpec((width, 1), lambda g, p: (0, 0)),
                pl.BlockSpec((1, tile), lambda g, p: (0, 0)),
                pl.BlockSpec((8, tile), lambda g, p: (0, 0)),
            ],
            out_specs=[
                pl.BlockSpec((block_rows, tile), lambda g, p: (0, 0)),
                pl.BlockSpec((8, block_rows), lambda g, p: (0, 0)),
            ],
            scratch_shapes=[
                pltpu.VMEM((width, width), jnp.bfloat16),
                pltpu.VMEM((width, tile), jnp.bfloat16),
            ],
        ),
        out_shape=[
            jax.ShapeDtypeStruct((block_rows, tile), jnp.float32),
            jax.ShapeDtypeStruct((8, block_rows), jnp.float32),
        ],
        compiler_params=pltpu.CompilerParams(vmem_limit_bytes=VMEM_BYTES),
    )(pos, packed, root_recip[:, None], rrow[None, :], jnp.broadcast_to(y[None, :], (8, tile)))


def add_body(count, in_ref, out_ref, slots, send_sem, recv_sem):
    me = lax.axis_index("obs")
    barrier = pltpu.get_barrier_semaphore()
    for k in range(1, count):
        pl.semaphore_signal(
            barrier, inc=1, device_id={"obs": lax.rem(me + k, count)}, device_id_type=pl.DeviceIdType.MESH
        )
    pl.semaphore_wait(barrier, count - 1)
    copies = []
    for k in range(1, count):
        copy = pltpu.make_async_remote_copy(
            src_ref=in_ref,
            dst_ref=slots.at[me],
            send_sem=send_sem.at[k],
            recv_sem=recv_sem.at[k],
            device_id={"obs": lax.rem(me + k, count)},
            device_id_type=pl.DeviceIdType.MESH,
        )
        copy.start()
        copies.append(copy)
    slots[me] = in_ref[...]
    for copy in copies:
        copy.wait()
    total = slots[0]
    for k in range(1, count):
        total = total + slots[k]
    out_ref[...] = total


def add_over_obs(values, count, collective_id):
    shape = values.shape
    flat = values.reshape(values.size // LANES, LANES)
    total = pl.pallas_call(
        functools.partial(add_body, count),
        out_shape=jax.ShapeDtypeStruct(flat.shape, flat.dtype),
        in_specs=[pl.BlockSpec(memory_space=pltpu.VMEM)],
        out_specs=pl.BlockSpec(memory_space=pltpu.VMEM),
        scratch_shapes=[
            pltpu.VMEM((count,) + flat.shape, flat.dtype),
            pltpu.SemaphoreType.DMA((count,)),
            pltpu.SemaphoreType.DMA((count,)),
        ],
        cost_estimate=pl.CostEstimate(
            flops=count * flat.size, bytes_accessed=400 * flat.size, transcendentals=0
        ),
        compiler_params=pltpu.CompilerParams(collective_id=collective_id, has_side_effects=True),
    )(flat)
    return total.reshape(shape)


def on_device(descriptors, candidates, sparse_index, targets, regularizer):
    obs_count = lax.axis_size("obs")
    sp_count = lax.axis_size("sp")
    obs_pos = lax.axis_index("obs")
    sp_pos = lax.axis_index("sp")
    width = sparse_index.shape[0]
    tile = width // obs_count
    share = -(-((obs_count // 2 + 1) * tile) // (sp_count * LANES)) * LANES
    normalizer = 24.0 * descriptors.shape[0] * obs_count

    normed = unit_rows(descriptors)
    table = lax.all_gather(unit_rows(candidates), "obs", axis=0, tiled=True)
    sparse = table.at[sparse_index].get(mode="promise_in_bounds")

    gram, sums = gram_call(
        sp_pos[None].astype(jnp.int32), normed, sparse, targets, obs_count, tile, share, sp_count
    )
    sums = add_over_obs(sums, obs_count, 0)
    part = lax.psum_scatter(gram, "obs", scatter_dimension=0, tiled=True)

    projected = sums[0] / math.sqrt(normalizer)
    root = lax.rsqrt(sums[1] / normalizer + regularizer)
    col_start = obs_pos * tile
    rrow = lax.dynamic_slice_in_dim(root, col_start, tile)
    window_start = col_start + sp_pos * share
    rwin = lax.dynamic_slice_in_dim(jnp.concatenate([root, root]), window_start, share)
    offset = sp_pos * share + lax.iota(jnp.int32, share)
    on_diag = lax.iota(jnp.int32, tile)[:, None] == offset[None, :]
    scaled = jnp.where(
        on_diag, 0.0, part.astype(jnp.float32) * (rrow[:, None] / normalizer) * rwin[None, :]
    ).astype(jnp.bfloat16)
    packed = lax.all_gather(scaled, ("obs", "sp"), axis=0, tiled=True)

    y = lax.dynamic_slice_in_dim(projected, col_start, tile)
    pos = jnp.stack([sp_pos, obs_pos]).astype(jnp.int32)
    inverse_tile, part_w = newton_call(
        pos, packed, root, rrow, y, obs_count, tile, share, sp_count
    )
    return inverse_tile, add_over_obs(part_w[0], obs_count, 1)


def solution(mesh):
    in_specs = (P("obs", None), P("obs", None), P(), P("obs"), P())
    out_specs = (P("sp", "obs"), P("sp"))
    return jax.shard_map(
        on_device, mesh=mesh, in_specs=in_specs, out_specs=out_specs, check_vma=False
    )
```

```python
import functools
import math

import jax
import jax.numpy as jnp
from jax import lax
from jax.experimental import pallas as pl
from jax.experimental.pallas import tpu as pltpu
from jax.sharding import PartitionSpec as P

epsilon = 1e-06
LANES = 128
VMEM_BYTES = 58 * 2**20


def unit_rows(row_block):
    values = row_block.astype(jnp.float32)
    return (values * lax.rsqrt(jnp.sum(values * values, axis=1, keepdims=True) + epsilon)).astype(
        jnp.bfloat16
    )


def gram_body(blocks, tile, share, ext, root, s_ref, norm_ref, sp_ref, tgt_ref, gram_ref, ws_ref, kext):
    step = pl.program_id(0)
    width = blocks * tile

    @pl.when(step < blocks)
    def _():
        inner = lax.dot_general(
            norm_ref[...], sp_ref[...], (((1,), (1,)), ((), ())), preferred_element_type=jnp.float32
        )
        scaled = inner * root
        squared = scaled * scaled
        kb = ((squared - 6.0) * squared + 3.0).astype(jnp.bfloat16)
        kext[:, pl.ds(pl.multiple_of(step * tile, tile), tile)] = kb

        @pl.when(step < ext)
        def _():
            kext[:, pl.ds(pl.multiple_of(width + step * tile, tile), tile)] = kb

        kf = kb.astype(jnp.float32)
        weighted = jnp.dot(tgt_ref[...], kb, preferred_element_type=jnp.float32)
        ws_ref[0:1, :] = weighted[0:1, :]
        ws_ref[1:2, :] = jnp.sum(kf * kf, axis=0, keepdims=True)

    @pl.when(step >= blocks)
    def _():
        j = step - blocks
        cols = pl.ds(pl.multiple_of(j * tile, tile), tile)
        window = pl.ds(pl.multiple_of(j * tile + s_ref[0] * share, LANES), share)
        gram_ref[...] = lax.dot_general(
            kext[:, cols], kext[:, window], (((0,), (0,)), ((), ())), preferred_element_type=jnp.float32
        ).astype(jnp.bfloat16)


def gram_call(s_pos, normed, sparse, targets, blocks, tile, share, sp_count):
    rows, depth = normed.shape
    width = blocks * tile
    ext = -(-((blocks - 1) * tile + sp_count * share - width) // tile)
    last = blocks - 1
    return pl.pallas_call(
        functools.partial(gram_body, blocks, tile, share, ext, math.sqrt(depth)),
        grid_spec=pltpu.PrefetchScalarGridSpec(
            num_scalar_prefetch=1,
            grid=(2 * blocks,),
            in_specs=[
                pl.BlockSpec((rows, depth), lambda g, s: (0, 0)),
                pl.BlockSpec((tile, depth), lambda g, s: (jnp.minimum(g, last), 0)),
                pl.BlockSpec((16, rows), lambda g, s: (0, 0)),
            ],
            out_specs=[
                pl.BlockSpec((tile, share), lambda g, s: (jnp.maximum(g - blocks, 0), 0)),
                pl.BlockSpec((2, tile), lambda g, s: (0, jnp.minimum(g, last))),
            ],
            scratch_shapes=[pltpu.VMEM((rows, width + ext * tile), jnp.bfloat16)],
        ),
        out_shape=[
            jax.ShapeDtypeStruct((width, share), jnp.bfloat16),
            jax.ShapeDtypeStruct((2, width), jnp.float32),
        ],
        compiler_params=pltpu.CompilerParams(vmem_limit_bytes=VMEM_BYTES),
    )(s_pos, normed, sparse, jnp.broadcast_to(targets[None, :], (16, rows)))


def newton_body(
    blocks, tile, share, sp_count, chunk, block_rows,
    pos_ref, packed_ref, rcol_ref, rrow_ref, y_ref, inv_ref, w_ref, dense, prod,
):
    step = pl.program_id(0)
    width = blocks * tile
    half = blocks // 2
    p_steps = width // chunk
    my_cols = pl.ds(pl.multiple_of(pos_ref[1] * tile, tile), tile)

    @pl.when(step < blocks)
    def _():
        rows = pl.ds(pl.multiple_of(step * tile, tile), tile)
        for s in range(sp_count):
            for q in range(share // LANES):
                offset = s * share + q * LANES
                if offset >= (half + 1) * tile:
                    continue
                col = lax.rem(step * tile + offset, width)
                cols = pl.ds(pl.multiple_of(col, LANES), LANES)
                block = packed_ref[s * tile : (s + 1) * tile, q * LANES : (q + 1) * LANES]
                dense[rows, cols] = block
                if tile <= offset < half * tile:
                    dense[cols, rows] = block.T

    @pl.when((step >= blocks) & (step < blocks + p_steps))
    def _():
        rows = pl.ds(pl.multiple_of((step - blocks) * chunk, chunk), chunk)
        prod[rows, :] = jnp.dot(
            dense[rows, :], dense[:, my_cols], preferred_element_type=jnp.float32
        ).astype(jnp.bfloat16)

    @pl.when(step >= blocks + p_steps)
    def _():
        local = pl.multiple_of((step - blocks - p_steps) * chunk, chunk)
        start = pl.multiple_of(pos_ref[0] * block_rows + local, chunk)
        rows = pl.ds(start, chunk)
        cubic = jnp.dot(dense[rows, :], prod[...], preferred_element_type=jnp.float32)
        on_diag = (start + lax.broadcasted_iota(jnp.int32, (chunk, tile), 0)) == (
            pos_ref[1] * tile + lax.broadcasted_iota(jnp.int32, (chunk, tile), 1)
        )
        series = (
            jnp.where(on_diag, 1.0, 0.0)
            - dense[rows, my_cols].astype(jnp.float32)
            + prod[rows, :].astype(jnp.float32)
            - cubic
        )
        out = series * rcol_ref[rows, :] * rrow_ref[...]
        inv_ref[pl.ds(local, chunk), :] = out
        w_ref[:, pl.ds(local, chunk)] = lax.dot_general(
            y_ref[...], out, (((1,), (1,)), ((), ())),
            precision=lax.Precision.HIGHEST, preferred_element_type=jnp.float32,
        )


def newton_call(pos, packed, root_recip, rrow, y, blocks, tile, share, sp_count):
    width = blocks * tile
    block_rows = width // sp_count
    chunk = min(512, block_rows)
    grid = blocks + width // chunk + block_rows // chunk
    last = blocks - 1
    return pl.pallas_call(
        functools.partial(newton_body, blocks, tile, share, sp_count, chunk, block_rows),
        grid_spec=pltpu.PrefetchScalarGridSpec(
            num_scalar_prefetch=1,
            grid=(grid,),
            in_specs=[
                pl.BlockSpec((sp_count * tile, share), lambda g, p: (jnp.minimum(g, last), 0)),
                pl.BlockSpec((width, 1), lambda g, p: (0, 0)),
                pl.BlockSpec((1, tile), lambda g, p: (0, 0)),
                pl.BlockSpec((8, tile), lambda g, p: (0, 0)),
            ],
            out_specs=[
                pl.BlockSpec((block_rows, tile), lambda g, p: (0, 0)),
                pl.BlockSpec((8, block_rows), lambda g, p: (0, 0)),
            ],
            scratch_shapes=[
                pltpu.VMEM((width, width), jnp.bfloat16),
                pltpu.VMEM((width, tile), jnp.bfloat16),
            ],
        ),
        out_shape=[
            jax.ShapeDtypeStruct((block_rows, tile), jnp.float32),
            jax.ShapeDtypeStruct((8, block_rows), jnp.float32),
        ],
        compiler_params=pltpu.CompilerParams(vmem_limit_bytes=VMEM_BYTES),
    )(pos, packed, root_recip[:, None], rrow[None, :], jnp.broadcast_to(y[None, :], (8, tile)))


def add_body(count, in_ref, out_ref, slots, send_sem, recv_sem):
    me = lax.axis_index("obs")
    barrier = pltpu.get_barrier_semaphore()
    for k in range(1, count):
        pl.semaphore_signal(
            barrier, inc=1, device_id={"obs": lax.rem(me + k, count)}, device_id_type=pl.DeviceIdType.MESH
        )
    pl.semaphore_wait(barrier, count - 1)
    copies = []
    for k in range(1, count):
        copy = pltpu.make_async_remote_copy(
            src_ref=in_ref,
            dst_ref=slots.at[me],
            send_sem=send_sem.at[k],
            recv_sem=recv_sem.at[k],
            device_id={"obs": lax.rem(me + k, count)},
            device_id_type=pl.DeviceIdType.MESH,
        )
        copy.start()
        copies.append(copy)
    slots[me] = in_ref[...]
    for copy in copies:
        copy.wait()
    total = slots[0]
    for k in range(1, count):
        total = total + slots[k]
    out_ref[...] = total


def add_over_obs(values, count, collective_id):
    shape = values.shape
    flat = values.reshape(values.size // LANES, LANES)
    total = pl.pallas_call(
        functools.partial(add_body, count),
        out_shape=jax.ShapeDtypeStruct(flat.shape, flat.dtype),
        in_specs=[pl.BlockSpec(memory_space=pltpu.VMEM)],
        out_specs=pl.BlockSpec(memory_space=pltpu.VMEM),
        scratch_shapes=[
            pltpu.VMEM((count,) + flat.shape, flat.dtype),
            pltpu.SemaphoreType.DMA((count,)),
            pltpu.SemaphoreType.DMA((count,)),
        ],
        cost_estimate=pl.CostEstimate(
            flops=count * flat.size, bytes_accessed=400 * flat.size, transcendentals=0
        ),
        compiler_params=pltpu.CompilerParams(collective_id=collective_id, has_side_effects=True),
    )(flat)
    return total.reshape(shape)


def spread_keys(z_count, sp_count):
    keys = [("z", k) for k in range(1, z_count)]
    for k in range(z_count):
        keys += [("x", k), ("core", k), ("core_x", k)]
        for d in range(1, sp_count):
            keys += [(name, k, d) for name in ("sp", "sp_a", "x_b", "core_sp", "core_a", "core_b")]
    return {key: place for place, key in enumerate(keys)}


def spread_body(z_count, sp_count, in_ref, out_ref, send_sem, recv_sem, own_sem):
    places = spread_keys(z_count, sp_count)
    obs = lax.axis_index("obs")
    s = lax.axis_index("sp")
    z, x, c = lax.div(obs, 4), lax.rem(lax.div(obs, 2), 2), lax.rem(obs, 2)
    half = in_ref.shape[0] // 2
    upper, lower = pl.ds(0, half), pl.ds(half, half)
    zs = [lax.bitwise_xor(z, k) for k in range(z_count)]
    to_sp = [lax.rem(s + d, sp_count) for d in range(sp_count)]
    from_sp = [lax.rem(s - d + sp_count, sp_count) for d in range(sp_count)]

    def device(z_to, x_to, c_to, s_to):
        return {"obs": z_to * 4 + x_to * 2 + c_to, "sp": s_to}

    def slot(z_of, x_of, s_of):
        return ((z_of * 2 + x_of) * 2 + c) * sp_count + s_of

    own_slot = slot(z, x, s)
    across, sibling = device(z, 1 - x, c, s), device(z, x, 1 - c, s)
    others = [device(zs[k], x, c, s) for k in range(1, z_count)]
    others += [device(z, x, c, to_sp[d]) for d in range(1, sp_count)]
    others += [across, sibling]
    barrier = pltpu.get_barrier_semaphore()
    for other in others:
        pl.semaphore_signal(barrier, inc=1, device_id=other, device_id_type=pl.DeviceIdType.MESH)
    pl.semaphore_wait(barrier, len(others))

    sent = {}

    def send(key, place, target, rows=None, own=False):
        src = in_ref if own else out_ref.at[place]
        dst = out_ref.at[place]
        if rows is not None:
            src, dst = src.at[rows], dst.at[rows]
        copy = pltpu.make_async_remote_copy(
            src_ref=src,
            dst_ref=dst,
            send_sem=send_sem.at[places[key]],
            recv_sem=recv_sem.at[places[key]],
            device_id=target,
            device_id_type=pl.DeviceIdType.MESH,
        )
        copy.start()
        sent[key] = copy

    keep = pltpu.make_async_copy(in_ref, out_ref.at[own_slot], own_sem)
    keep.start()
    for k in range(1, z_count):
        send(("z", k), own_slot, others[k - 1], own=True)

    def fan_out(k):
        place = slot(zs[k], x, s)
        send(("x", k), place, across, own=k == 0)
        for d in range(1, sp_count):
            send(("sp", k, d), place, device(z, x, c, to_sp[d]), own=k == 0)
        send(("core", k), place, sibling, own=k == 0)

    def relay(k):
        sent[("x", k)].wait_recv()
        place = slot(zs[k], 1 - x, s)
        for d in range(1, sp_count):
            send(("sp_a", k, d), place, device(z, x, c, to_sp[d]), upper)
        send(("core_x", k), place, sibling)
        for d in range(1, sp_count):
            sent[("sp", k, d)].wait_recv()
            place = slot(zs[k], x, from_sp[d])
            send(("x_b", k, d), place, across, lower)
            send(("core_sp", k, d), place, sibling)

    def finish(k):
        for d in range(1, sp_count):
            place = slot(zs[k], 1 - x, from_sp[d])
            sent[("sp_a", k, d)].wait_recv()
            send(("core_a", k, d), place, sibling, upper)
            sent[("x_b", k, d)].wait_recv()
            send(("core_b", k, d), place, sibling, lower)

    fan_out(0)
    for k in range(1, z_count):
        sent[("z", k)].wait_recv()
        fan_out(k)
        relay(k - 1)
        if k > 1:
            finish(k - 2)
    relay(z_count - 1)
    if z_count > 1:
        finish(z_count - 2)
    finish(z_count - 1)
    keep.wait()
    for key, copy in sent.items():
        copy.wait_send()
        if key[0].startswith("core"):
            copy.wait_recv()


def spread(shard, obs_count, sp_count, collective_id):
    rows, cols = shard.shape
    z_count = obs_count // 4
    total = obs_count * sp_count
    sems = len(spread_keys(z_count, sp_count))
    gathered = pl.pallas_call(
        functools.partial(spread_body, z_count, sp_count),
        out_shape=jax.ShapeDtypeStruct((total, rows, cols), shard.dtype),
        in_specs=[pl.BlockSpec(memory_space=pl.ANY)],
        out_specs=pl.BlockSpec(memory_space=pl.ANY),
        scratch_shapes=[
            pltpu.SemaphoreType.DMA((sems,)),
            pltpu.SemaphoreType.DMA((sems,)),
            pltpu.SemaphoreType.DMA,
        ],
        compiler_params=pltpu.CompilerParams(collective_id=collective_id, has_side_effects=True),
    )(shard)
    return gathered.reshape(total * rows, cols)


def on_device(descriptors, candidates, sparse_index, targets, regularizer):
    obs_count = lax.axis_size("obs")
    sp_count = lax.axis_size("sp")
    obs_pos = lax.axis_index("obs")
    sp_pos = lax.axis_index("sp")
    width = sparse_index.shape[0]
    tile = width // obs_count
    share = -(-((obs_count // 2 + 1) * tile) // (sp_count * LANES)) * LANES
    normalizer = 24.0 * descriptors.shape[0] * obs_count

    normed = unit_rows(descriptors)
    piece = candidates.shape[0] // sp_count
    own = lax.dynamic_slice_in_dim(candidates, sp_pos * piece, piece)
    table = spread(unit_rows(own), obs_count, sp_count, 2)
    sparse = table.at[sparse_index].get(mode="promise_in_bounds")

    gram, sums = gram_call(
        sp_pos[None].astype(jnp.int32), normed, sparse, targets, obs_count, tile, share, sp_count
    )
    sums = add_over_obs(sums, obs_count, 0)
    part = lax.psum_scatter(gram, "obs", scatter_dimension=0, tiled=True)

    projected = sums[0] / math.sqrt(normalizer)
    root = lax.rsqrt(sums[1] / normalizer + regularizer)
    col_start = obs_pos * tile
    rrow = lax.dynamic_slice_in_dim(root, col_start, tile)
    window_start = col_start + sp_pos * share
    rwin = lax.dynamic_slice_in_dim(jnp.concatenate([root, root]), window_start, share)
    offset = sp_pos * share + lax.iota(jnp.int32, share)
    on_diag = lax.iota(jnp.int32, tile)[:, None] == offset[None, :]
    scaled = jnp.where(
        on_diag, 0.0, part.astype(jnp.float32) * (rrow[:, None] / normalizer) * rwin[None, :]
    ).astype(jnp.bfloat16)
    packed = spread(scaled, obs_count, sp_count, 3)

    y = lax.dynamic_slice_in_dim(projected, col_start, tile)
    pos = jnp.stack([sp_pos, obs_pos]).astype(jnp.int32)
    inverse_tile, part_w = newton_call(
        pos, packed, root, rrow, y, obs_count, tile, share, sp_count
    )
    return inverse_tile, add_over_obs(part_w[0], obs_count, 1)


def solution(mesh):
    in_specs = (P("obs", None), P("obs", None), P(), P("obs"), P())
    out_specs = (P("sp", "obs"), P("sp"))
    return jax.shard_map(
        on_device, mesh=mesh, in_specs=in_specs, out_specs=out_specs, check_vma=False
    )
```

```python
import functools
import math

import jax
import jax.numpy as jnp
from jax import lax
from jax.experimental import pallas as pl
from jax.experimental.pallas import tpu as pltpu
from jax.sharding import PartitionSpec as P

epsilon = 1e-06
LANES = 128
VMEM_BYTES = 58 * 2**20


def unit_rows(row_block):
    values = row_block.astype(jnp.float32)
    return (values * lax.rsqrt(jnp.sum(values * values, axis=1, keepdims=True) + epsilon)).astype(
        jnp.bfloat16
    )


def gram_body(
    blocks, tile, share, first, ext, root, s_ref, norm_ref, sp_ref, tgt_ref, gram_ref, late_ref, ws_ref, kext
):
    step = pl.program_id(0)
    width = blocks * tile

    @pl.when(step < blocks)
    def _():
        inner = lax.dot_general(
            norm_ref[...], sp_ref[...], (((1,), (1,)), ((), ())), preferred_element_type=jnp.float32
        )
        scaled = inner * root
        squared = scaled * scaled
        kb = ((squared - 6.0) * squared + 3.0).astype(jnp.bfloat16)
        kext[:, pl.ds(pl.multiple_of(step * tile, tile), tile)] = kb

        @pl.when(step < ext)
        def _():
            kext[:, pl.ds(pl.multiple_of(width + step * tile, tile), tile)] = kb

        kf = kb.astype(jnp.float32)
        weighted = jnp.dot(tgt_ref[...], kb, preferred_element_type=jnp.float32)
        ws_ref[0:1, :] = weighted[0:1, :]
        ws_ref[1:2, :] = jnp.sum(kf * kf, axis=0, keepdims=True)

    @pl.when(step >= blocks)
    def _():
        j = step - blocks
        cols = pl.ds(pl.multiple_of(j * tile, tile), tile)
        window = pl.ds(pl.multiple_of(j * tile + s_ref[0] * share, LANES), share)
        product = lax.dot_general(
            kext[:, cols], kext[:, window], (((0,), (0,)), ((), ())), preferred_element_type=jnp.float32
        ).astype(jnp.bfloat16)
        gram_ref[...] = product[:, :first]
        late_ref[...] = product[:, first:]


def gram_call(s_pos, normed, sparse, targets, blocks, tile, share, first, sp_count):
    rows, depth = normed.shape
    width = blocks * tile
    ext = -(-((blocks - 1) * tile + sp_count * share - width) // tile)
    last = blocks - 1
    return pl.pallas_call(
        functools.partial(gram_body, blocks, tile, share, first, ext, math.sqrt(depth)),
        grid_spec=pltpu.PrefetchScalarGridSpec(
            num_scalar_prefetch=1,
            grid=(2 * blocks,),
            in_specs=[
                pl.BlockSpec((rows, depth), lambda g, s: (0, 0)),
                pl.BlockSpec((tile, depth), lambda g, s: (jnp.minimum(g, last), 0)),
                pl.BlockSpec((16, rows), lambda g, s: (0, 0)),
            ],
            out_specs=[
                pl.BlockSpec((tile, first), lambda g, s: (jnp.maximum(g - blocks, 0), 0)),
                pl.BlockSpec((tile, share - first), lambda g, s: (jnp.maximum(g - blocks, 0), 0)),
                pl.BlockSpec((2, tile), lambda g, s: (0, jnp.minimum(g, last))),
            ],
            scratch_shapes=[pltpu.VMEM((rows, width + ext * tile), jnp.bfloat16)],
        ),
        out_shape=[
            jax.ShapeDtypeStruct((width, first), jnp.bfloat16),
            jax.ShapeDtypeStruct((width, share - first), jnp.bfloat16),
            jax.ShapeDtypeStruct((2, width), jnp.float32),
        ],
        compiler_params=pltpu.CompilerParams(vmem_limit_bytes=VMEM_BYTES),
    )(s_pos, normed, sparse, jnp.broadcast_to(targets[None, :], (16, rows)))


def newton_body(
    blocks, tile, share, first, sp_count, chunk, block_rows,
    pos_ref, packed_ref, late_ref, rcol_ref, rrow_ref, y_ref, inv_ref, w_ref, dense, prod,
):
    step = pl.program_id(0)
    width = blocks * tile
    half = blocks // 2
    p_steps = width // chunk
    my_cols = pl.ds(pl.multiple_of(pos_ref[1] * tile, tile), tile)

    @pl.when(step < blocks)
    def _():
        rows = pl.ds(pl.multiple_of(step * tile, tile), tile)
        for s in range(sp_count):
            for q in range(share // LANES):
                offset = s * share + q * LANES
                if offset >= (half + 1) * tile:
                    continue
                col = lax.rem(step * tile + offset, width)
                cols = pl.ds(pl.multiple_of(col, LANES), LANES)
                source, at = (packed_ref, q * LANES) if q * LANES < first else (late_ref, q * LANES - first)
                block = source[s * tile : (s + 1) * tile, at : at + LANES]
                dense[rows, cols] = block
                if tile <= offset < half * tile:
                    dense[cols, rows] = block.T

    @pl.when((step >= blocks) & (step < blocks + p_steps))
    def _():
        rows = pl.ds(pl.multiple_of((step - blocks) * chunk, chunk), chunk)
        prod[rows, :] = jnp.dot(
            dense[rows, :], dense[:, my_cols], preferred_element_type=jnp.float32
        ).astype(jnp.bfloat16)

    @pl.when(step >= blocks + p_steps)
    def _():
        local = pl.multiple_of((step - blocks - p_steps) * chunk, chunk)
        start = pl.multiple_of(pos_ref[0] * block_rows + local, chunk)
        rows = pl.ds(start, chunk)
        cubic = jnp.dot(dense[rows, :], prod[...], preferred_element_type=jnp.float32)
        on_diag = (start + lax.broadcasted_iota(jnp.int32, (chunk, tile), 0)) == (
            pos_ref[1] * tile + lax.broadcasted_iota(jnp.int32, (chunk, tile), 1)
        )
        series = (
            jnp.where(on_diag, 1.0, 0.0)
            - dense[rows, my_cols].astype(jnp.float32)
            + prod[rows, :].astype(jnp.float32)
            - cubic
        )
        out = series * rcol_ref[rows, :] * rrow_ref[...]
        inv_ref[pl.ds(local, chunk), :] = out
        w_ref[:, pl.ds(local, chunk)] = lax.dot_general(
            y_ref[...], out, (((1,), (1,)), ((), ())),
            precision=lax.Precision.HIGHEST, preferred_element_type=jnp.float32,
        )


def newton_call(pos, packed, late, root_recip, rrow, y, blocks, tile, share, first, sp_count):
    width = blocks * tile
    block_rows = width // sp_count
    chunk = min(512, block_rows)
    grid = blocks + width // chunk + block_rows // chunk
    last = blocks - 1
    return pl.pallas_call(
        functools.partial(newton_body, blocks, tile, share, first, sp_count, chunk, block_rows),
        grid_spec=pltpu.PrefetchScalarGridSpec(
            num_scalar_prefetch=1,
            grid=(grid,),
            in_specs=[
                pl.BlockSpec((sp_count * tile, first), lambda g, p: (jnp.minimum(g, last), 0)),
                pl.BlockSpec((sp_count * tile, share - first), lambda g, p: (jnp.minimum(g, last), 0)),
                pl.BlockSpec((width, 1), lambda g, p: (0, 0)),
                pl.BlockSpec((1, tile), lambda g, p: (0, 0)),
                pl.BlockSpec((8, tile), lambda g, p: (0, 0)),
            ],
            out_specs=[
                pl.BlockSpec((block_rows, tile), lambda g, p: (0, 0)),
                pl.BlockSpec((8, block_rows), lambda g, p: (0, 0)),
            ],
            scratch_shapes=[
                pltpu.VMEM((width, width), jnp.bfloat16),
                pltpu.VMEM((width, tile), jnp.bfloat16),
            ],
        ),
        out_shape=[
            jax.ShapeDtypeStruct((block_rows, tile), jnp.float32),
            jax.ShapeDtypeStruct((8, block_rows), jnp.float32),
        ],
        compiler_params=pltpu.CompilerParams(vmem_limit_bytes=VMEM_BYTES),
    )(pos, packed, late, root_recip[:, None], rrow[None, :], jnp.broadcast_to(y[None, :], (8, tile)))


def add_body(count, in_ref, out_ref, slots, send_sem, recv_sem):
    me = lax.axis_index("obs")
    barrier = pltpu.get_barrier_semaphore()
    for k in range(1, count):
        pl.semaphore_signal(
            barrier, inc=1, device_id={"obs": lax.rem(me + k, count)}, device_id_type=pl.DeviceIdType.MESH
        )
    pl.semaphore_wait(barrier, count - 1)
    copies = []
    for k in range(1, count):
        copy = pltpu.make_async_remote_copy(
            src_ref=in_ref,
            dst_ref=slots.at[me],
            send_sem=send_sem.at[k],
            recv_sem=recv_sem.at[k],
            device_id={"obs": lax.rem(me + k, count)},
            device_id_type=pl.DeviceIdType.MESH,
        )
        copy.start()
        copies.append(copy)
    slots[me] = in_ref[...]
    for copy in copies:
        copy.wait()
    total = slots[0]
    for k in range(1, count):
        total = total + slots[k]
    out_ref[...] = total


def add_over_obs(values, count, collective_id):
    shape = values.shape
    flat = values.reshape(values.size // LANES, LANES)
    total = pl.pallas_call(
        functools.partial(add_body, count),
        out_shape=jax.ShapeDtypeStruct(flat.shape, flat.dtype),
        in_specs=[pl.BlockSpec(memory_space=pltpu.VMEM)],
        out_specs=pl.BlockSpec(memory_space=pltpu.VMEM),
        scratch_shapes=[
            pltpu.VMEM((count,) + flat.shape, flat.dtype),
            pltpu.SemaphoreType.DMA((count,)),
            pltpu.SemaphoreType.DMA((count,)),
        ],
        cost_estimate=pl.CostEstimate(
            flops=count * flat.size, bytes_accessed=400 * flat.size, transcendentals=0
        ),
        compiler_params=pltpu.CompilerParams(collective_id=collective_id, has_side_effects=True),
    )(flat)
    return total.reshape(shape)


def spread_keys(z_count, sp_count):
    keys = [("z", k) for k in range(1, z_count)]
    for k in range(z_count):
        keys += [("x", k), ("core", k), ("core_x", k)]
        for d in range(1, sp_count):
            keys += [(name, k, d) for name in ("sp", "sp_a", "x_b", "core_sp", "core_a", "core_b")]
    return {key: place for place, key in enumerate(keys)}


def spread_body(z_count, sp_count, in_ref, out_ref, send_sem, recv_sem, own_sem):
    places = spread_keys(z_count, sp_count)
    obs = lax.axis_index("obs")
    s = lax.axis_index("sp")
    z, x, c = lax.div(obs, 4), lax.rem(lax.div(obs, 2), 2), lax.rem(obs, 2)
    half = in_ref.shape[0] // 2
    upper, lower = pl.ds(0, half), pl.ds(half, half)
    zs = [lax.bitwise_xor(z, k) for k in range(z_count)]
    to_sp = [lax.rem(s + d, sp_count) for d in range(sp_count)]
    from_sp = [lax.rem(s - d + sp_count, sp_count) for d in range(sp_count)]

    def device(z_to, x_to, c_to, s_to):
        return {"obs": z_to * 4 + x_to * 2 + c_to, "sp": s_to}

    def slot(z_of, x_of, s_of):
        return ((z_of * 2 + x_of) * 2 + c) * sp_count + s_of

    own_slot = slot(z, x, s)
    across, sibling = device(z, 1 - x, c, s), device(z, x, 1 - c, s)
    others = [device(zs[k], x, c, s) for k in range(1, z_count)]
    others += [device(z, x, c, to_sp[d]) for d in range(1, sp_count)]
    others += [across, sibling]
    barrier = pltpu.get_barrier_semaphore()
    for other in others:
        pl.semaphore_signal(barrier, inc=1, device_id=other, device_id_type=pl.DeviceIdType.MESH)
    pl.semaphore_wait(barrier, len(others))

    sent = {}

    def send(key, place, target, rows=None, own=False):
        src = in_ref if own else out_ref.at[place]
        dst = out_ref.at[place]
        if rows is not None:
            src, dst = src.at[rows], dst.at[rows]
        copy = pltpu.make_async_remote_copy(
            src_ref=src,
            dst_ref=dst,
            send_sem=send_sem.at[places[key]],
            recv_sem=recv_sem.at[places[key]],
            device_id=target,
            device_id_type=pl.DeviceIdType.MESH,
        )
        copy.start()
        sent[key] = copy

    keep = pltpu.make_async_copy(in_ref, out_ref.at[own_slot], own_sem)
    keep.start()
    for k in range(1, z_count):
        send(("z", k), own_slot, others[k - 1], own=True)

    def fan_out(k):
        place = slot(zs[k], x, s)
        send(("x", k), place, across, own=k == 0)
        for d in range(1, sp_count):
            send(("sp", k, d), place, device(z, x, c, to_sp[d]), own=k == 0)
        send(("core", k), place, sibling, own=k == 0)

    def relay(k):
        sent[("x", k)].wait_recv()
        place = slot(zs[k], 1 - x, s)
        for d in range(1, sp_count):
            send(("sp_a", k, d), place, device(z, x, c, to_sp[d]), upper)
        send(("core_x", k), place, sibling)
        for d in range(1, sp_count):
            sent[("sp", k, d)].wait_recv()
            place = slot(zs[k], x, from_sp[d])
            send(("x_b", k, d), place, across, lower)
            send(("core_sp", k, d), place, sibling)

    def finish(k):
        for d in range(1, sp_count):
            place = slot(zs[k], 1 - x, from_sp[d])
            sent[("sp_a", k, d)].wait_recv()
            send(("core_a", k, d), place, sibling, upper)
            sent[("x_b", k, d)].wait_recv()
            send(("core_b", k, d), place, sibling, lower)

    fan_out(0)
    for k in range(1, z_count):
        sent[("z", k)].wait_recv()
        fan_out(k)
        relay(k - 1)
        if k > 1:
            finish(k - 2)
    relay(z_count - 1)
    if z_count > 1:
        finish(z_count - 2)
    finish(z_count - 1)
    keep.wait()
    for key, copy in sent.items():
        copy.wait_send()
        if key[0].startswith("core"):
            copy.wait_recv()


def spread(shard, obs_count, sp_count, collective_id):
    rows, cols = shard.shape
    z_count = obs_count // 4
    total = obs_count * sp_count
    sems = len(spread_keys(z_count, sp_count))
    gathered = pl.pallas_call(
        functools.partial(spread_body, z_count, sp_count),
        out_shape=jax.ShapeDtypeStruct((total, rows, cols), shard.dtype),
        in_specs=[pl.BlockSpec(memory_space=pl.ANY)],
        out_specs=pl.BlockSpec(memory_space=pl.ANY),
        scratch_shapes=[
            pltpu.SemaphoreType.DMA((sems,)),
            pltpu.SemaphoreType.DMA((sems,)),
            pltpu.SemaphoreType.DMA,
        ],
        cost_estimate=pl.CostEstimate(
            flops=0, bytes_accessed=16 * total * rows * cols, transcendentals=0
        ),
        compiler_params=pltpu.CompilerParams(collective_id=collective_id, has_side_effects=True),
    )(shard)
    return gathered.reshape(total * rows, cols)


def on_device(descriptors, candidates, sparse_index, targets, regularizer):
    obs_count = lax.axis_size("obs")
    sp_count = lax.axis_size("sp")
    obs_pos = lax.axis_index("obs")
    sp_pos = lax.axis_index("sp")
    width = sparse_index.shape[0]
    tile = width // obs_count
    share = -(-((obs_count // 2 + 1) * tile) // (sp_count * LANES)) * LANES
    normalizer = 24.0 * descriptors.shape[0] * obs_count

    normed = unit_rows(descriptors)
    piece = candidates.shape[0] // sp_count
    own = lax.dynamic_slice_in_dim(candidates, sp_pos * piece, piece)
    table = spread(unit_rows(own), obs_count, sp_count, 2)
    sparse = table.at[sparse_index].get(mode="promise_in_bounds")

    first = -(-share // (2 * LANES)) * LANES
    gram, late_gram, sums = gram_call(
        sp_pos[None].astype(jnp.int32), normed, sparse, targets, obs_count, tile, share, first, sp_count
    )
    sums = add_over_obs(sums, obs_count, 0)
    part = lax.psum_scatter(gram, "obs", scatter_dimension=0, tiled=True)
    late_part = lax.psum_scatter(late_gram, "obs", scatter_dimension=0, tiled=True)

    projected = sums[0] / math.sqrt(normalizer)
    root = lax.rsqrt(sums[1] / normalizer + regularizer)
    col_start = obs_pos * tile
    rrow = lax.dynamic_slice_in_dim(root, col_start, tile)
    window_start = col_start + sp_pos * share
    rwin = lax.dynamic_slice_in_dim(jnp.concatenate([root, root]), window_start, share)
    offset = sp_pos * share + lax.iota(jnp.int32, share)
    on_diag = lax.iota(jnp.int32, tile)[:, None] == offset[None, :]
    row_scale = rrow[:, None] / normalizer

    def scale(block, cols):
        scaled = block.astype(jnp.float32) * row_scale * rwin[None, cols]
        return jnp.where(on_diag[:, cols], 0.0, scaled).astype(jnp.bfloat16)

    packed = spread(scale(part, slice(0, first)), obs_count, sp_count, 3)
    late = spread(scale(late_part, slice(first, share)), obs_count, sp_count, 4)

    y = lax.dynamic_slice_in_dim(projected, col_start, tile)
    pos = jnp.stack([sp_pos, obs_pos]).astype(jnp.int32)
    inverse_tile, part_w = newton_call(
        pos, packed, late, root, rrow, y, obs_count, tile, share, first, sp_count
    )
    return inverse_tile, add_over_obs(part_w[0], obs_count, 1)


def solution(mesh):
    in_specs = (P("obs", None), P("obs", None), P(), P("obs"), P())
    out_specs = (P("sp", "obs"), P("sp"))
    return jax.shard_map(
        on_device, mesh=mesh, in_specs=in_specs, out_specs=out_specs, check_vma=False
    )
```
